32 devices in a mesh: groups: 2 (over y), seq: 8 (over z, x), cache: 2 (over core).
Axes of the slice: x: 2, y: 2, z: 4, core: 2. Of those that a mesh axis runs over, the one named last changes fastest.
Arguments:
- queries: bfloat16 [128, 2048, 128], P('groups', ('seq', 'cache')), parts along dimension 0, may hold values from -8 to 8
- stretch_keys: bfloat16 [128, 2048, 128], P('groups', 'seq'), parts along dimension 0, may hold values from -8 to 8
- stretch_values: bfloat16 [128, 2048, 128], P('groups', 'seq'), parts along dimension 0, may hold values from -6 to 6
- cache_keys: bfloat16 [128, 2048, 128], P(('groups', 'seq'), 'cache'), parts along dimension 0, may hold values from -6 to 6
- cache_values: bfloat16 [128, 2048, 128], P(('groups', 'seq'), 'cache'), parts along dimension 0, may hold values from -6 to 6
- rand_blocks: int32 [32, 3], P('groups'), parts along dimension 0, may hold values from 2 to 28, as said below
Outputs:
- attended: bfloat16 [128, 2048, 128], P('groups', ('seq', 'cache')), parts along dimension 0
The draws below stay inside these ranges and needn't reach their ends.
There are 2 independent parts, one for each index of `groups`. The reference program is written for one: setup_inputs(seed, part) draws one part's arguments, and reference() takes and returns one part's arrays. A program takes and returns all parts, laid end to end along the dimension named above; each array names one. Nothing has to cross between parts.
Inputs may be any that keep to these rules, and one draw needn't show every extreme that they name: `rand_blocks`: row i holds 3 different block numbers, each at least 2 and below 16 + i - 2.
All inputs are finite; a program needn't handle non-finite values.
Results may differ from the reference program's by a relative error of at most 0.0049.
Values may be sent and summed in bfloat16 or wider, within the bound.
A program may use at most 128 MiB of HBM per device.

```python
import math
import jax
import jax.numpy as jnp
from jax import lax

DH = 128
BLK = 128
NR = 3
CB = 16
L = 2048
QB = 16
CLEN = 2048
PAIRS = 64


def draw_queries(key, part):
    sample = jnp.clip(jax.random.normal(jax.random.fold_in(key, 1), (PAIRS, L, DH), jnp.float32), -4.5, 4.5)
    return sample.astype(jnp.bfloat16)


def draw_stretch_keys(key, part):
    sample = jnp.clip(jax.random.normal(jax.random.fold_in(key, 2), (PAIRS, L, DH), jnp.float32), -4.5, 4.5)
    return sample.astype(jnp.bfloat16)


def draw_rand_blocks(key, part):
    block_index = jnp.arange(QB, dtype=jnp.int32)[:, None]
    column = jnp.arange(NR, dtype=jnp.int32)[None, :]
    span = CB + block_index - 4
    stratum = span // NR
    drawn = jax.random.randint(key, (QB, NR), 0, 1 << 20, dtype=jnp.int32) % stratum
    drawn = jnp.where((block_index == 0) & (column == 0), 0, drawn)
    drawn = jnp.where((block_index == QB - 1) & (column == NR - 1), stratum - 1, drawn)
    return 2 + column * stratum + drawn


def steps_of(rng, dims, split, low, largest):
    factor_of, own = 1.0, jax.random.fold_in(rng, 6)
    for dim, shards_of in split:
        draws = jnp.exp(jax.random.uniform(jax.random.fold_in(own, dim), (shards_of,), jnp.float32, low / len(split), largest / len(split)))
        factor_of = factor_of * jnp.repeat(draws, dims[dim] // shards_of).reshape([-1 if axis == dim else 1 for axis in range(len(dims))])
    return factor_of


def normal_values(rng, shape, spread, reach, pieces=(), kind=jnp.bfloat16):
    level = steps_of(rng, shape, pieces, -0.22, 0.18) if pieces else 1.0
    entries = jax.random.normal(rng, shape, jnp.float32) * spread * level
    return jnp.minimum(jnp.maximum(entries, -reach), reach).astype(kind)


def setup_inputs(seed: int = 0, part: int = 0) -> dict:
    keys = jax.random.split(jax.random.key(seed), 7)
    own_keys = jax.random.split(jax.random.fold_in(keys[6], part), 7)
    queries = draw_queries(jax.random.fold_in(jax.random.fold_in(keys[6], part), 71), part)
    stretch_keys = draw_stretch_keys(jax.random.fold_in(jax.random.fold_in(keys[6], part), 71), part)
    stretch_values = normal_values(own_keys[2], (PAIRS, L, DH), 1.0, 6.0, ((1, 8),))
    cache_keys = normal_values(own_keys[3], (PAIRS, CLEN, DH), 1.0, 6.0, ((0, 8), (1, 2)))
    cache_values = normal_values(own_keys[4], (PAIRS, CLEN, DH), 1.0, 6.0, ((0, 8), (1, 2)))
    rand_blocks = draw_rand_blocks(jax.random.fold_in(jax.random.fold_in(keys[6], part), 71), part)
    return dict(queries=queries, stretch_keys=stretch_keys, stretch_values=stretch_values, cache_keys=cache_keys, cache_values=cache_values, rand_blocks=rand_blocks)


def block_lists(rand_blocks):
    block_count = rand_blocks.shape[0]
    starts = jnp.arange(block_count, dtype=jnp.int32)[:, None] + CB
    window = starts + jnp.array([-2, -1, 0], jnp.int32)[None, :]
    anchors = jnp.broadcast_to(jnp.array([0, 1], jnp.int32)[None, :], (block_count, 2))
    return jnp.concatenate([window, anchors, rand_blocks.astype(jnp.int32)], axis=1)

def attend_blocks(query_blocks, key_lists, key_blocks, value_blocks):
    groups, block_width, head_width = query_blocks.shape
    listed = key_lists.shape[1]
    chosen_keys = jnp.take(key_blocks, key_lists, axis=0).reshape(groups, listed * block_width, head_width)
    chosen_values = jnp.take(value_blocks, key_lists, axis=0).reshape(groups, listed * block_width, head_width)
    scores = jnp.einsum('gqd,gkd->gqk', query_blocks.astype(jnp.float32), chosen_keys.astype(jnp.float32))
    scores = scores * (1.0 / math.sqrt(head_width))
    key_slot = jnp.arange(listed * block_width, dtype=jnp.int32)
    query_slot = jnp.arange(block_width, dtype=jnp.int32)
    blocked = (key_slot // block_width == 2)[None, :] & ((key_slot % block_width)[None, :] > query_slot[:, None])
    scores = jnp.where(blocked[None], -jnp.inf, scores)
    row_max = lax.optimization_barrier(jnp.max(scores, axis=2, keepdims=True))
    weights = jnp.exp(scores - row_max)
    row_probs = (weights / lax.optimization_barrier(jnp.sum(weights, axis=2, keepdims=True))).astype(jnp.bfloat16)
    result = jnp.einsum('gqk,gkd->gqd', row_probs.astype(jnp.float32), chosen_values.astype(jnp.float32))
    return result.astype(jnp.bfloat16)

def reference(queries, stretch_keys, stretch_values, cache_keys, cache_values, rand_blocks):
    key_lists = block_lists(rand_blocks)

    def one_pair(operands):
        query_rows, key_rows, value_rows, prefix_key, prefix_value = operands
        key_blocks = jnp.concatenate([prefix_key, key_rows], axis=0).reshape(-1, BLK, DH)
        value_blocks = jnp.concatenate([prefix_value, value_rows], axis=0).reshape(-1, BLK, DH)
        result = attend_blocks(query_rows.reshape(QB, BLK, DH), key_lists, key_blocks, value_blocks)
        return result.reshape(L, DH)
    return lax.map(one_pair, (queries, stretch_keys, stretch_values, cache_keys, cache_values))
```

```python
import functools
import math

import jax
import jax.numpy as jnp
from jax import lax
from jax.experimental import pallas as pl
from jax.experimental.pallas import tpu as pltpu
from jax.sharding import PartitionSpec as P

BLK = 128
CB = 16
LINE = 2
HIDDEN = -1e30
MESH = pl.DeviceIdType.MESH


def fused_kernel(
    chips, pairs, split, rand_ref, q_hbm, k_hbm, v_hbm, ck_hbm, cv_hbm, out_hbm, *scratch
):
    helped = chips // 2 // LINE * split
    take = iter(scratch)
    q_bufs, k_bufs, v_bufs, o_bufs = ([next(take) for _ in range(pairs)] for _ in range(4))
    hq_bufs, hk_bufs, hv_bufs, ho_bufs = ([next(take) for _ in range(helped)] for _ in range(4))
    l_bufs = [next(take) for _ in range(split)]
    hl_buf, part_a, part_b, lse_a, lse_b, merged = (next(take) for _ in range(6))
    q_in, k_in, v_in, hq_in, hk_in, hv_in = (next(take) for _ in range(6))
    (
        q_out, k_out, v_out, ks_out, vs_out, ck_out, cv_out, o_out, o_in, low_in,
        hk_out, hv_out, hq_out, hq_down, l_out, ho_out, hl_out,
        a_in, b_in, la_in, lb_in, m_out,
    ) = (next(take) for _ in range(22))

    s = lax.axis_index("seq")
    c = lax.axis_index("cache")
    per_device = q_hbm.shape[1]
    per_chip = k_hbm.shape[1]
    side_blocks = ck_hbm.shape[1]
    cached = 2 * side_blocks
    head_width = q_hbm.shape[3]
    mine = 2 * s + c
    devices = 2 * chips
    middle = chips // 2
    half_blocks = middle * per_chip
    upper = s // middle
    own_first = cached + upper * half_blocks
    helper = middle - LINE + upper * LINE
    is_helper = (s >= middle - LINE) & (s < middle + LINE)

    barrier = pltpu.get_barrier_semaphore()

    def greet(d, carry):
        other = (mine + d) % devices
        pl.semaphore_signal(
            barrier,
            inc=1,
            device_id={"seq": other // 2, "cache": other % 2},
            device_id_type=MESH,
        )
        return carry

    lax.fori_loop(1, devices, greet, 0)
    pl.semaphore_wait(barrier, devices - 1)

    def remote(src, dst, send, recv, s2, c2):
        pltpu.make_async_remote_copy(
            src_ref=src,
            dst_ref=dst,
            send_sem=send,
            recv_sem=recv,
            device_id={"seq": s2, "cache": c2},
            device_id_type=MESH,
        ).start()

    def local(src, dst, sem):
        pltpu.make_async_copy(src, dst, sem).start()

    def await_bytes(ref, sem):
        pltpu.make_async_copy(ref, ref, sem).wait()

    stretch_at = pl.ds(cached + s * per_chip, per_chip)
    query_at = pl.ds(mine * per_device, per_device)
    half_at = pl.ds((s % middle) * per_chip, per_chip)

    def spread(p):
        def queries_to(s2):
            same = (2 * s2 + c) * pairs + p
            cross = (2 * s2 + 1 - c) * pairs + p
            remote(q_hbm.at[same], q_bufs[p].at[query_at], q_out, q_in.at[p], s2, c)
            remote(q_hbm.at[cross], q_bufs[p].at[query_at], q_out, q_in.at[p], s2, 1 - c)

        def keys_to(s2, k_sem, v_sem):
            same = (2 * s2 + c) * pairs + p
            remote(k_hbm.at[same], k_bufs[p].at[stretch_at], k_sem, k_in.at[p], s2, c)
            remote(v_hbm.at[same], v_bufs[p].at[stretch_at], v_sem, v_in.at[p], s2, c)

        if p < split:

            def to_half(d, carry):
                keys_to(upper * middle + (s + d) % middle, ks_out, vs_out)
                return carry

            def to_chip(d, carry):
                queries_to((s + d) % chips)
                return carry

            lax.fori_loop(1, chips, to_chip, 0)
            lax.fori_loop(1, middle, to_half, 0)
        else:

            def to_chip(d, carry):
                s2 = (s + d) % chips
                keys_to(s2, k_out, v_out)
                queries_to(s2)
                return carry

            lax.fori_loop(1, chips, to_chip, 0)
        own = mine * pairs + p
        cross = (2 * s + 1 - c) * pairs + p
        side = pl.ds(c * side_blocks, side_blocks)
        give = (1 - c) * pairs + p
        keep = c * pairs + p
        remote(ck_hbm.at[give], k_bufs[p].at[side], ck_out, k_in.at[p], s, 1 - c)
        remote(cv_hbm.at[give], v_bufs[p].at[side], cv_out, v_in.at[p], s, 1 - c)
        remote(q_hbm.at[cross], q_bufs[p].at[query_at], q_out, q_in.at[p], s, 1 - c)
        local(q_hbm.at[own], q_bufs[p].at[query_at], q_in.at[p])
        local(k_hbm.at[own], k_bufs[p].at[stretch_at], k_in.at[p])
        local(v_hbm.at[own], v_bufs[p].at[stretch_at], v_in.at[p])
        local(ck_hbm.at[keep], k_bufs[p].at[side], k_in.at[p])
        local(cv_hbm.at[keep], v_bufs[p].at[side], v_in.at[p])

    def head_of(side_upper, x, side, u):
        home = (1 - side_upper) * middle + (u // split) * LINE + x
        return (2 * home + side) * pairs + u % split

    def spread_help(u):
        for x in range(LINE):
            target = helper + x
            away = s != target
            for side in range(2):
                head = head_of(upper, x, side, u)

                @pl.when(away | (c != side))
                def _():
                    remote(q_hbm.at[head], hq_bufs[u].at[query_at], hq_out, hq_in.at[u], target, side)

                @pl.when(jnp.logical_not(away) & (c == side))
                def _():
                    local(q_hbm.at[head], hq_bufs[u].at[query_at], hq_in.at[u])

                @pl.when(upper == 1)
                def _():
                    remote(
                        q_hbm.at[head_of(0, x, side, u)],
                        hq_bufs[u].at[query_at],
                        hq_down,
                        hq_in.at[u],
                        middle - LINE + x,
                        side,
                    )

            same = head_of(upper, x, c, u)

            @pl.when(away)
            def _():
                remote(k_hbm.at[same], hk_bufs[u].at[half_at], hk_out, hk_in.at[u], target, c)
                remote(v_hbm.at[same], hv_bufs[u].at[half_at], hv_out, hv_in.at[u], target, c)

            @pl.when(jnp.logical_not(away))
            def _():
                local(k_hbm.at[same], hk_bufs[u].at[half_at], hk_in.at[u])
                local(v_hbm.at[same], hv_bufs[u].at[half_at], hv_in.at[u])

    factor = math.log2(math.e) / math.sqrt(head_width)
    row_at = lax.broadcasted_iota(jnp.int32, (BLK, BLK), 0)
    col_at = lax.broadcasted_iota(jnp.int32, (BLK, BLK), 1)
    later = col_at > row_at

    def joined(tiles):
        return tiles.reshape(-1, head_width)

    def softmax_sum(query, keys_of, values_of, shown):
        scores = [
            lax.dot_general(
                query, tile, (((1,), (1,)), ((), ())), preferred_element_type=jnp.float32
            )
            for tile in keys_of()
        ]
        scores[0] = jnp.where(later, HIDDEN, scores[0])
        if shown is not None:
            scores = [
                score if show is None else jnp.where(show, score, HIDDEN)
                for score, show in zip(scores, shown)
            ]
        top = functools.reduce(
            jnp.maximum, [jnp.max(score, axis=1, keepdims=True) for score in scores]
        )
        weights = [jnp.exp2((score - top) * factor) for score in scores]
        total = sum(jnp.sum(weight, axis=1, keepdims=True) for weight in weights)
        result = sum(
            jnp.dot(weight.astype(jnp.bfloat16), tile, preferred_element_type=jnp.float32)
            for weight, tile in zip(weights, values_of())
        )
        return (result / total).astype(jnp.bfloat16), top * factor + jnp.log2(total)

    def attend(p, i):
        def listed(buffer):
            first = cached + i
            tiles = [buffer[first], joined(buffer[pl.ds(first - 2, 2)]), joined(buffer[0:2])]
            return tiles + [buffer[rand_ref[n, i]] for n in range(rand_ref.shape[0])]

        result, _ = softmax_sum(
            q_bufs[p][i], lambda: listed(k_bufs[p]), lambda: listed(v_bufs[p]), None
        )
        o_bufs[p][i] = result

    def in_half(b):
        return (b >= own_first) & (b < own_first + half_blocks)

    def as_rows(lse):
        return jnp.broadcast_to(lse, (BLK, BLK)).T[0:1]

    def attend_home(p, i):
        numbers = [cached + i, cached + i - 2, cached + i - 1]
        numbers += [rand_ref[n, i] for n in range(rand_ref.shape[0])]
        shown = [(b < cached) | in_half(b) for b in numbers]
        places = [jnp.where(show, b, 0) for show, b in zip(shown, numbers)]

        def listed(buffer):
            return [buffer[place] for place in places] + [joined(buffer[0:2])]

        result, lse = softmax_sum(
            q_bufs[p][i],
            lambda: listed(k_bufs[p]),
            lambda: listed(v_bufs[p]),
            shown + [None],
        )
        o_bufs[p][i] = result
        l_bufs[p][i] = as_rows(lse)

    def attend_help(u, i):
        numbers = [cached + i, cached + i - 2, cached + i - 1]
        numbers += [rand_ref[n, i] for n in range(rand_ref.shape[0])]
        shown = [in_half(b) for b in numbers]
        places = [jnp.where(show, b - own_first, 0) for show, b in zip(shown, numbers)]

        def listed(buffer):
            return [buffer[place] for place in places]

        result, lse = softmax_sum(
            hq_bufs[u][i], lambda: listed(hk_bufs[u]), lambda: listed(hv_bufs[u]), shown
        )
        ho_bufs[u][i] = result
        hl_buf[u, i] = as_rows(lse)

    def each_block(target, act):
        def block_step(n, inner):
            act(target * per_device + n)
            return inner

        lax.fori_loop(0, per_device, block_step, 0)

    def blocks_at(target):
        return pl.ds(target * per_device, per_device)

    def put(src, dst, send, recv, target):
        @pl.when(target != mine)
        def _():
            remote(src, dst, send, recv, target // 2, target % 2)

        @pl.when(target == mine)
        def _():
            local(src, dst, recv)

    def direct_head(p):
        await_bytes(q_bufs[p], q_in.at[p])
        await_bytes(k_bufs[p], k_in.at[p])
        await_bytes(v_bufs[p], v_in.at[p])
        head = mine * pairs + p

        def device_step(d, carry):
            target = (mine + d) % devices
            each_block(target, lambda i: attend(p, i))
            put(o_bufs[p].at[blocks_at(target)], out_hbm.at[head], o_out, o_in, target)
            return carry

        lax.fori_loop(1, devices + 1, device_step, 0)

    def split_head(p):
        came = cached + half_blocks
        await_bytes(q_bufs[p], q_in.at[p])
        await_bytes(k_bufs[p].at[pl.ds(0, came)], k_in.at[p])
        await_bytes(v_bufs[p].at[pl.ds(0, came)], v_in.at[p])
        head = mine * pairs + p
        place = mine * split + p

        def device_step(d, carry):
            target = (mine + d) % devices
            whole = (upper == 0) & (target < chips)
            each_block(target, lambda i: attend_home(p, i))

            @pl.when(whole)
            def _():
                put(o_bufs[p].at[blocks_at(target)], out_hbm.at[head], o_out, low_in, target)

            @pl.when(jnp.logical_not(whole))
            def _():
                put(o_bufs[p].at[blocks_at(target)], part_a.at[place], o_out, a_in, target)
                put(l_bufs[p].at[blocks_at(target)], lse_a.at[place], l_out, la_in, target)

            return carry

        lax.fori_loop(1, devices + 1, device_step, 0)

    def help_head(u):
        @pl.when(upper == 0)
        def _():
            await_bytes(hq_bufs[u], hq_in.at[u])

        @pl.when(upper == 1)
        def _():
            await_bytes(hq_bufs[u].at[pl.ds(0, half_blocks)], hq_in.at[u])

        await_bytes(hk_bufs[u], hk_in.at[u])
        await_bytes(hv_bufs[u], hv_in.at[u])
        home = (1 - upper) * middle + (u // split) * LINE + (s - helper)
        place = (2 * home + c) * split + u % split

        def serve(target):
            each_block(target, lambda i: attend_help(u, i))
            put(ho_bufs[u].at[blocks_at(target)], part_b.at[place], ho_out, b_in, target)
            put(hl_buf.at[u, blocks_at(target)], lse_b.at[place], hl_out, lb_in, target)

        def device_step(d, carry):
            target = (mine + d) % devices

            @pl.when((upper == 0) | (target >= chips))
            def _():
                serve(target)

            return carry

        lax.fori_loop(1, devices + 1, device_step, 0)

    places = devices * split

    def merge():
        def waits(n):
            await_bytes(part_a.at[pl.ds(0, n)], a_in)
            await_bytes(part_b.at[pl.ds(0, n)], b_in)
            await_bytes(lse_a.at[pl.ds(0, n)], la_in)
            await_bytes(lse_b.at[pl.ds(0, n)], lb_in)

        def blend(place, carry):
            for n in range(per_device):

                def spread_out(ref):
                    return jnp.broadcast_to(ref[place, n], (BLK, BLK)).T

                left, right = spread_out(lse_a), spread_out(lse_b)
                top = jnp.maximum(left, right)
                left, right = jnp.exp2(left - top), jnp.exp2(right - top)
                both = part_a[place, n].astype(jnp.float32) * left
                both += part_b[place, n].astype(jnp.float32) * right
                merged[place, n] = (both / (left + right)).astype(jnp.bfloat16)
            local(
                merged.at[place], out_hbm.at[place // split * pairs + place % split], m_out
            )
            return carry

        @pl.when(upper == 0)
        def _():
            waits(places // 2)
            lax.fori_loop(places // 2, places, blend, 0)

        @pl.when(upper == 1)
        def _():
            waits(places)
            lax.fori_loop(0, places, blend, 0)

    def help_all():
        @pl.when(is_helper)
        def _():
            for u in range(helped):
                help_head(u)

    def spread_helps():
        for u in range(helped):
            spread_help(u)

    order = [(lambda p=p: spread(p), lambda p=p: split_head(p)) for p in range(split)]
    order.append((spread_helps, help_all))
    order += [(lambda p=p: spread(p), lambda p=p: direct_head(p)) for p in range(split, pairs)]
    ahead = 3
    for send, _ in order[:ahead]:
        send()
    for n, (_, work) in enumerate(order):
        if n + ahead < len(order):
            order[n + ahead][0]()
        work()
    merge()

    def blocks(n):
        return q_hbm.at[pl.ds(0, n)]

    def chunks(n):
        return k_hbm.at[pl.ds(0, n)]

    others = devices - 1
    await_bytes(out_hbm.at[pl.ds(0, devices * (pairs - split))], o_in)
    await_bytes(blocks(others * pairs), q_out)
    await_bytes(blocks(others * pairs), o_out)
    await_bytes(chunks((chips - 1) * (pairs - split)), k_out)
    await_bytes(chunks((chips - 1) * (pairs - split)), v_out)
    await_bytes(chunks((middle - 1) * split), ks_out)
    await_bytes(chunks((middle - 1) * split), vs_out)
    await_bytes(ck_hbm.at[pl.ds(0, pairs)], ck_out)
    await_bytes(cv_hbm.at[pl.ds(0, pairs)], cv_out)

    @pl.when(is_helper)
    def _():
        await_bytes(chunks((LINE - 1) * helped), hk_out)
        await_bytes(chunks((LINE - 1) * helped), hv_out)
        await_bytes(blocks((2 * LINE - 1) * helped), hq_out)

        @pl.when(upper == 0)
        def _():
            await_bytes(chunks(others * helped // 2), ho_out)
            await_bytes(hl_buf.at[:, pl.ds(0, others * per_device)], hl_out)

        @pl.when(upper == 1)
        def _():
            await_bytes(chunks((chips - 1) * helped // 2), ho_out)
            await_bytes(hl_buf.at[:, pl.ds(0, (chips - 1) * per_device)], hl_out)

    @pl.when(jnp.logical_not(is_helper))
    def _():
        await_bytes(chunks(LINE * helped), hk_out)
        await_bytes(chunks(LINE * helped), hv_out)
        await_bytes(blocks(2 * LINE * helped), hq_out)

    @pl.when(upper == 0)
    def _():
        await_bytes(blocks(chips * split), low_in)
        await_bytes(merged.at[pl.ds(0, places // 2)], m_out)
        await_bytes(lse_a.at[pl.ds(0, chips * split)], l_out)

    @pl.when(upper == 1)
    def _():
        await_bytes(blocks(2 * LINE * helped), hq_down)
        await_bytes(merged, m_out)
        await_bytes(lse_a.at[pl.ds(0, others * split)], l_out)


def heads_apart(queries, stretch_keys, stretch_values, cache_keys, cache_values, rand_blocks):
    chips = lax.axis_size("seq")
    pairs = cache_keys.shape[0] // 2
    split = pairs // 2
    helped = chips // 2 // LINE * split
    per_device = queries.shape[1] // BLK
    length = 2 * chips * queries.shape[1]
    keys = 2 * cache_keys.shape[1] + length
    width = queries.shape[2]

    def blocked(array):
        return array.reshape(array.shape[0], -1, BLK, width)

    def buffer(size, count):
        return [pltpu.VMEM((size // BLK, BLK, width), jnp.bfloat16)] * count

    places = 2 * chips * split
    part = pltpu.VMEM((places, per_device, BLK, width), jnp.bfloat16)
    lse = pltpu.VMEM((places, per_device, 1, BLK), jnp.float32)
    buffers = buffer(length, pairs) + buffer(keys, 2 * pairs) + buffer(length, pairs)
    buffers += buffer(length, helped) + buffer(length // 2, 2 * helped) + buffer(length, helped)
    buffers += [pltpu.VMEM((length // BLK, 1, BLK), jnp.float32)] * split
    buffers += [pltpu.VMEM((helped, length // BLK, 1, BLK), jnp.float32)]
    buffers += [part, part, lse, lse, part]
    anywhere = pl.BlockSpec(memory_space=pl.ANY)
    attended = pl.pallas_call(
        functools.partial(fused_kernel, chips, pairs, split),
        out_shape=jax.ShapeDtypeStruct(blocked(queries).shape, queries.dtype),
        in_specs=[pl.BlockSpec(memory_space=pltpu.SMEM)] + [anywhere] * 5,
        out_specs=anywhere,
        scratch_shapes=buffers
        + [pltpu.SemaphoreType.DMA((pairs,))] * 3
        + [pltpu.SemaphoreType.DMA((helped,))] * 3
        + [pltpu.SemaphoreType.DMA(())] * 22,
        compiler_params=pltpu.CompilerParams(collective_id=0, has_side_effects=True),
    )(
        rand_blocks.T,
        blocked(queries),
        blocked(stretch_keys),
        blocked(stretch_values),
        blocked(cache_keys),
        blocked(cache_values),
    )
    return attended.reshape(queries.shape)


def block_lists(rand_blocks):
    block_count = rand_blocks.shape[0]
    starts = jnp.arange(block_count, dtype=jnp.int32)[:, None] + CB
    window = starts + jnp.array([-2, -1, 0], jnp.int32)[None, :]
    anchors = jnp.broadcast_to(jnp.array([0, 1], jnp.int32)[None, :], (block_count, 2))
    return jnp.concatenate([window, anchors, rand_blocks], axis=1)


def attend_blocks(query_blocks, key_lists, key_blocks, value_blocks):
    groups, block_width, head_width = query_blocks.shape
    listed = key_lists.shape[1]
    chosen_keys = jnp.take(key_blocks, key_lists, axis=0).reshape(
        groups, listed * block_width, head_width
    )
    chosen_values = jnp.take(value_blocks, key_lists, axis=0).reshape(
        groups, listed * block_width, head_width
    )
    scores = jnp.einsum(
        "gqd,gkd->gqk", query_blocks, chosen_keys, preferred_element_type=jnp.float32
    )
    scores = scores * (1.0 / math.sqrt(head_width))
    key_slot = jnp.arange(listed * block_width, dtype=jnp.int32)
    query_slot = jnp.arange(block_width, dtype=jnp.int32)
    blocked = (key_slot // block_width == 2)[None, :] & (
        (key_slot % block_width)[None, :] > query_slot[:, None]
    )
    scores = jnp.where(blocked[None], -jnp.inf, scores)
    row_max = jnp.max(scores, axis=2, keepdims=True)
    weights = jnp.exp(scores - row_max)
    row_probs = (weights / jnp.sum(weights, axis=2, keepdims=True)).astype(jnp.bfloat16)
    result = jnp.einsum(
        "gqk,gkd->gqd", row_probs, chosen_values, preferred_element_type=jnp.float32
    )
    return result.astype(jnp.bfloat16)


def rows_apart(queries, stretch_keys, stretch_values, cache_keys, cache_values, rand_blocks):
    local_rows = queries.shape[1]
    head_width = queries.shape[2]
    seq_devices = lax.axis_size("seq")
    cache_devices = lax.axis_size("cache")
    cache_side = lax.axis_index("cache")
    query_heads, key_heads, value_heads = (
        lax.all_to_all(queries, "seq", split_axis=0, concat_axis=1, tiled=True),
        lax.all_to_all(stretch_keys, "seq", split_axis=0, concat_axis=1, tiled=True),
        lax.all_to_all(stretch_values, "seq", split_axis=0, concat_axis=1, tiled=True),
    )
    prefix_keys, prefix_values = (
        lax.all_gather(cache_keys, "cache", axis=1, tiled=True),
        lax.all_gather(cache_values, "cache", axis=1, tiled=True),
    )
    all_lists = block_lists(rand_blocks)
    per_segment = local_rows // BLK
    my_blocks = seq_devices * per_segment
    block_order = jnp.arange(my_blocks, dtype=jnp.int32)
    global_block = (
        block_order // per_segment * cache_devices + cache_side
    ) * per_segment + block_order % per_segment
    my_lists = jnp.take(all_lists, global_block, axis=0)
    group_size = math.gcd(my_blocks, max(1, 2048 // BLK))
    group_count = my_blocks // group_size
    lists_grouped = my_lists.reshape(group_count, group_size, my_lists.shape[1])

    def one_pair(operands):
        query_rows, key_rows, value_rows, prefix_key, prefix_value = operands
        key_blocks = jnp.concatenate([prefix_key, key_rows], axis=0).reshape(-1, BLK, head_width)
        value_blocks = jnp.concatenate([prefix_value, value_rows], axis=0).reshape(
            -1, BLK, head_width
        )
        query_groups = query_rows.reshape(group_count, group_size, BLK, head_width)

        def one_group(group_operands):
            query_group, list_group = group_operands
            return attend_blocks(query_group, list_group, key_blocks, value_blocks)

        result = lax.map(one_group, (query_groups, lists_grouped))
        return result.reshape(my_blocks * BLK, head_width)

    attended_heads = lax.map(
        one_pair, (query_heads, key_heads, value_heads, prefix_keys, prefix_values)
    )
    return lax.all_to_all(attended_heads, "seq", split_axis=1, concat_axis=0, tiled=True)


def per_device(queries, stretch_keys, stretch_values, cache_keys, cache_values, rand_blocks):
    if cache_keys.shape[0] % 4 == 0 and lax.axis_size("seq") % (2 * LINE) == 0:
        plan = heads_apart
    else:
        plan = rows_apart
    return plan(queries, stretch_keys, stretch_values, cache_keys, cache_values, rand_blocks)


def solution(mesh):
    placed = (
        P("groups", ("seq", "cache"), None),
        P("groups", "seq", None),
        P("groups", "seq", None),
        P(("groups", "seq"), "cache", None),
        P(("groups", "seq"), "cache", None),
        P("groups", None),
    )
    return jax.shard_map(
        per_device,
        mesh=mesh,
        in_specs=placed,
        out_specs=P("groups", ("seq", "cache"), None),
        check_vma=False,
    )
```
